32 devices in a mesh: tile: 8 (over z, y), head: 4 (over x, core).
Axes of the slice: x: 2, y: 2, z: 4, core: 2. Of those that a mesh axis runs over, the one named last changes fastest.
Arguments:
- tokens: bfloat16 [256, 32768], P('head', 'tile'), may hold values from -6 to 6
- grad_in: bfloat16 [256, 32768], P('head', 'tile'), may hold values from -6 to 6
- w_qkv: bfloat16 [3, 256, 256], P(None, 'head'), may hold values from -0.375 to 0.375
- w_out: bfloat16 [256, 256], P('head'), may hold values from -0.375 to 0.375
- neighbors: int32 [9, 32768], P(None, 'tile'), may hold values from 0 to 4479, as said below
- send_rows: int32 [8, 3, 128], P('tile'), may hold values from 0 to 4096, as said below
Outputs:
- d_tokens: float32 [256, 32768], P('head', 'tile')
- grad_qkv: float32 [3, 256, 256], P(None, 'head')
- grad_out: float32 [256, 256], P('head')
The draws below stay inside these ranges and needn't reach their ends.
Inputs may be any that keep to these rules, and one draw needn't show every extreme that they name: `send_rows`: entries of list p of index d are rows of index d, live entries first, the rest equal to 4096; list 2 of every index is full, and list 0 of index 0 is half full. `neighbors`: slot 0 of row r of an index is r itself; an entry below 4096 lies within 64 rows of r, counted around the index's 4096 rows; every entry at or above 4096 points to a live entry of the list it names.
All inputs are finite; a program needn't handle non-finite values.
Results may differ from the reference program's by a relative error of at most 0.0059.
Values may be sent and summed in bfloat16 or wider, within the bound.
A program may use at most 64 MiB of HBM per device.

```python
import math
import jax
import jax.numpy as jnp
from jax import lax

C = 256
HEADS = 8
NBR = 9
ROWS_DEV = 4096
BORDER = 128
GROUPS = 8
ROWS = 32768


def border_counts(key):
    counts = jax.random.randint(jax.random.fold_in(key, 11), (GROUPS, 3), BORDER // 2, BORDER + 1)
    counts = counts.at[:, 2].set(BORDER)
    counts = counts.at[0, 0].set(BORDER // 2)
    return counts.astype(jnp.int32)


def draw_send_rows(key, part):
    counts = border_counts(key)
    subkeys = jax.random.split(jax.random.fold_in(key, 23), GROUPS * 3)
    chosen = jax.vmap(lambda subkey: jax.random.permutation(subkey, ROWS_DEV)[:BORDER])(subkeys)
    chosen = chosen.reshape(GROUPS, 3, BORDER)
    column = jnp.arange(BORDER, dtype=jnp.int32)
    return jnp.where(column[None, None, :] < counts[:, :, None], chosen, ROWS_DEV).astype(jnp.int32)


def draw_neighbors(key, part):
    counts = border_counts(key)
    first, second, third, fourth = jax.random.split(jax.random.fold_in(key, 37), 4)
    shape = (NBR - 1, GROUPS, ROWS_DEV)
    row_ids = jnp.arange(ROWS_DEV, dtype=jnp.int32)
    local = (row_ids[None, None, :] + jax.random.randint(first, shape, -64, 65)) % ROWS_DEV
    peer = jax.random.randint(second, shape, 0, 3)
    device = jnp.arange(GROUPS, dtype=jnp.int32)[None, :, None]
    offsets = jnp.array([1, GROUPS - 1, GROUPS // 2], dtype=jnp.int32)
    source = (device - offsets[peer]) % GROUPS
    live = counts[source, peer]
    column = jax.random.randint(third, shape, 0, BORDER) % live
    remote = ROWS_DEV + peer * BORDER + column
    picked = jax.random.randint(fourth, shape, 0, 8) == 0
    entries = jnp.where(picked, remote, local)
    entries = entries.at[NBR - 2, :, 0].set(ROWS_DEV + 3 * BORDER - 1)
    selfrow = jnp.broadcast_to(row_ids[None, None, :], (1, GROUPS, ROWS_DEV))
    whole = jnp.concatenate([selfrow, entries], axis=0)
    return whole.reshape(NBR, GROUPS * ROWS_DEV).astype(jnp.int32)


def block_levels(stream_key, extent, pieces, low, largest):
    loudness, own = 1.0, jax.random.fold_in(stream_key, 6)
    for dim, parts in pieces:
        heights = jnp.exp(jax.random.uniform(jax.random.fold_in(own, dim), (parts,), jnp.float32, low / len(pieces), largest / len(pieces)))
        loudness = loudness * jnp.repeat(heights, extent[dim] // parts).reshape([-1 if axis == dim else 1 for axis in range(len(extent))])
    return loudness


def gaussian(stream_key, shape, width, limit, shards=(), kind=jnp.bfloat16):
    level = block_levels(stream_key, shape, shards, -0.22, 0.18) if shards else 1.0
    values = jax.random.normal(stream_key, shape, jnp.float32) * width * level
    return jnp.minimum(jnp.maximum(values, -limit), limit).astype(kind)


def setup_inputs(seed: int = 0) -> dict:
    streams_of = jax.random.split(jax.random.key(seed), 7)
    return {
        "tokens": gaussian(streams_of[0], (C, ROWS), 1.0, 6.0, ((0, 4), (1, 8))),
        "grad_in": gaussian(streams_of[1], (C, ROWS), 1.0, 6.0, ((0, 4), (1, 8))),
        "w_qkv": gaussian(streams_of[2], (3, C, C), C ** -0.5, 0.375, ((1, 4),)),
        "w_out": gaussian(streams_of[3], (C, C), C ** -0.5, 0.375, ((0, 4),)),
        "neighbors": draw_neighbors(jax.random.fold_in(streams_of[6], 71), 0),
        "send_rows": draw_send_rows(jax.random.fold_in(streams_of[6], 71), 0),
    }


def reference(tokens, grad_in, w_qkv, w_out, neighbors, send_rows):
    total_rows = GROUPS * ROWS_DEV
    head_dim = C // HEADS
    score_scale = 1.0 / math.sqrt(head_dim)
    devices = jnp.arange(GROUPS, dtype=jnp.int32)
    offsets = jnp.array([1, GROUPS - 1, GROUPS // 2], dtype=jnp.int32)
    sources = (devices[:, None] - offsets[None, :]) % GROUPS
    lists = send_rows[sources, jnp.arange(3, dtype=jnp.int32)[None, :], :]
    remote = jnp.where(lists < ROWS_DEV, sources[:, :, None] * ROWS_DEV + lists, total_rows).astype(jnp.int32)
    own_rows = devices[:, None] * ROWS_DEV + jnp.arange(ROWS_DEV, dtype=jnp.int32)[None, :]
    mapping = jnp.concatenate([own_rows, remote.reshape(GROUPS, 3 * BORDER)], axis=1)
    local_table = neighbors.reshape(NBR, GROUPS, ROWS_DEV)
    table = mapping[devices[None, :, None], local_table].reshape(NBR, total_rows).astype(jnp.int32)
    x_rows = tokens.T
    dy_rows = grad_in.T
    query = jnp.dot(x_rows, w_qkv[0].T, preferred_element_type=jnp.float32).astype(jnp.bfloat16)
    keys = jnp.dot(x_rows, w_qkv[1].T, preferred_element_type=jnp.float32).astype(jnp.bfloat16)
    values = jnp.dot(x_rows, w_qkv[2].T, preferred_element_type=jnp.float32).astype(jnp.bfloat16)
    packed = jnp.concatenate([keys, values], axis=1)
    padded = jnp.concatenate([packed, jnp.zeros((1, 2 * C), jnp.bfloat16)], axis=0)
    grad_att = jnp.dot(dy_rows, w_out.T, preferred_element_type=jnp.float32)

    def block_step(totals, block_index):
        start = (block_index * ROWS_DEV).astype(jnp.int32)
        picks = lax.dynamic_slice_in_dim(table, start, ROWS_DEV, 1)
        near = padded[picks].astype(jnp.float32)
        near_keys = near[:, :, :C].reshape(NBR, ROWS_DEV, HEADS, head_dim)
        near_values = near[:, :, C:].reshape(NBR, ROWS_DEV, HEADS, head_dim)
        query_rows = lax.dynamic_slice_in_dim(query, start, ROWS_DEV, 0).astype(jnp.float32).reshape(ROWS_DEV, HEADS, head_dim)
        dout_rows = lax.dynamic_slice_in_dim(grad_att, start, ROWS_DEV, 0).reshape(ROWS_DEV, HEADS, head_dim)
        scores = jnp.einsum('rhd,jrhd->jrh', query_rows, near_keys) * score_scale
        expon = jnp.exp(scores)
        probs = expon / lax.optimization_barrier(jnp.sum(expon, axis=0))
        attended = jnp.einsum('jrh,jrhd->rhd', probs, near_values)
        dprob = jnp.einsum('rhd,jrhd->jrh', dout_rows, near_values)
        dscore = probs * (dprob - lax.optimization_barrier(jnp.sum(probs * dprob, axis=0)))
        grad_query = jnp.einsum('jrh,jrhd->rhd', dscore, near_keys) * score_scale
        grad_keys = dscore[..., None] * query_rows[None] * score_scale
        grad_values = probs[..., None] * dout_rows[None]
        grad_near = jnp.concatenate([grad_keys.reshape(NBR, ROWS_DEV, C), grad_values.reshape(NBR, ROWS_DEV, C)], axis=2)
        totals = totals.at[picks.reshape(-1)].add(grad_near.reshape(NBR * ROWS_DEV, 2 * C))
        return (totals, (attended.reshape(ROWS_DEV, C).astype(jnp.bfloat16), grad_query.reshape(ROWS_DEV, C)))
    totals, (attended, grad_query) = lax.scan(block_step, jnp.zeros((total_rows + 1, 2 * C), jnp.float32), jnp.arange(GROUPS, dtype=jnp.int32))
    attended = attended.reshape(total_rows, C)
    grad_q = grad_query.reshape(total_rows, C).astype(jnp.bfloat16)
    grad_k = totals[:total_rows, :C].astype(jnp.bfloat16)
    grad_v = totals[:total_rows, C:].astype(jnp.bfloat16)
    d_rows = dy_rows.astype(jnp.float32) + jnp.dot(grad_q, w_qkv[0], preferred_element_type=jnp.float32) + jnp.dot(grad_k, w_qkv[1], preferred_element_type=jnp.float32) + jnp.dot(grad_v, w_qkv[2], preferred_element_type=jnp.float32)
    grad_scale = 1.0 / math.sqrt(total_rows)
    grad_qkv = jnp.stack([jnp.dot(grad_q.T, x_rows, preferred_element_type=jnp.float32), jnp.dot(grad_k.T, x_rows, preferred_element_type=jnp.float32), jnp.dot(grad_v.T, x_rows, preferred_element_type=jnp.float32)]) * grad_scale
    grad_out = jnp.dot(attended.T, dy_rows, preferred_element_type=jnp.float32) * grad_scale
    return (d_rows.T, grad_qkv, grad_out)
```

```python
import functools
import math

import jax
import jax.numpy as jnp
from jax import lax
from jax.experimental import pallas as pl
from jax.experimental.pallas import tpu as pltpu
from jax.sharding import PartitionSpec as P

C = 256
HEADS = 8
NBR = 9
MARGIN = 64
BLOCK = 2 * MARGIN
WINDOW = 2 * BLOCK
NEVER = -1.0e30

NT = (((1,), (1,)), ((), ()))
TN = (((0,), (0,)), ((), ()))


def mm(a, b, dims=(((1,), (0,)), ((), ()))):
    return lax.dot_general(a, b, dims, preferred_element_type=jnp.float32)


def passed_along(value, axis, steps):
    count = lax.axis_size(axis)
    pairs = [(source, (source + steps) % count) for source in range(count)]
    return lax.ppermute(value, axis, pairs)


def attention_body(
    rows, near, keys, grad_scale,
    recv, picks, out,
    q_s, g_s, k_s, kt_s, v_s, vt_s, kw, ktw, vw, vtw, qbd, gbd, p_all, ds_all, gk_s, gv_s, att_s, gq_s,
):
    head_dim = C // HEADS
    scale = 1.0 / math.sqrt(head_dim)
    scale2 = scale / math.log(2.0)
    wide = keys - near + WINDOW
    at_dy = keys
    at_w = keys + rows
    bf16 = jnp.bfloat16

    def weight(t):
        return recv[:, at_w + t * C : at_w + (t + 1) * C]

    q_ext = mm(weight(0), recv[:, :near])
    q_s[...] = pltpu.roll(q_ext, near - MARGIN, 1)[:, :rows].astype(bf16)
    g_s[...] = mm(weight(3), recv[:, at_dy : at_dy + rows]).astype(bf16)
    kt = mm(weight(1), recv[:, :keys])
    kt_s[...] = kt.astype(bf16)
    k_s[...] = kt.T.astype(bf16)
    vt = mm(weight(2), recv[:, :keys])
    vt_s[...] = vt.astype(bf16)
    v_s[...] = vt.T.astype(bf16)
    kw[WINDOW:, :] = k_s[near:, :]
    vw[WINDOW:, :] = v_s[near:, :]
    ktw[:, WINDOW:] = kt_s[:, near:]
    vtw[:, WINDOW:] = vt_s[:, near:]
    qbd[...] = jnp.zeros_like(qbd)
    gbd[...] = jnp.zeros_like(gbd)
    gk_s[...] = jnp.zeros_like(gk_s)
    gv_s[...] = jnp.zeros_like(gv_s)
    gq_s[:, rows:] = jnp.zeros((C, near - rows), jnp.float32)

    def block(b, carry):
        start = pl.multiple_of(b * BLOCK, BLOCK)
        cols = pl.ds(start, BLOCK)
        span = pl.ds(start, WINDOW)
        kw[:WINDOW, :] = k_s[span, :]
        vw[:WINDOW, :] = v_s[span, :]
        ktw[:, :WINDOW] = kt_s[:, span]
        vtw[:, :WINDOW] = vt_s[:, span]
        for h in range(HEADS):
            chan = slice(h * head_dim, (h + 1) * head_dim)
            lane = slice(h * BLOCK, (h + 1) * BLOCK)
            qbd[chan, lane] = q_s[chan, cols]
            gbd[chan, lane] = g_s[chan, cols]
        ids = lax.broadcasted_iota(jnp.int32, (wide, BLOCK), 0)
        count = jnp.zeros((wide, BLOCK), jnp.float32)
        for j in range(NBR):
            count = count + jnp.where(ids == picks[j : j + 1, cols], 1.0, 0.0)
        bias = jnp.where(count > 0.0, jnp.log2(jnp.maximum(count, 1.0)), NEVER)
        bias = jnp.concatenate([bias, bias], axis=1)
        for pair in range(HEADS // 2):
            lane = slice(pair * 2 * BLOCK, (pair + 1) * 2 * BLOCK)
            chan = slice(pair * 2 * head_dim, (pair + 1) * 2 * head_dim)
            low = slice(pair * 2 * head_dim, pair * 2 * head_dim + head_dim)
            high = slice(pair * 2 * head_dim + head_dim, (pair + 1) * 2 * head_dim)
            expon = jnp.exp2(mm(kw[...], qbd[:, lane]) * scale2 + bias)
            total = jnp.sum(expon, axis=0, keepdims=True)
            prob = expon * (1.0 / total)
            dprob = mm(vw[...], gbd[:, lane])
            mean = jnp.sum(prob * dprob, axis=0, keepdims=True)
            dscore = (prob * (dprob - mean)).astype(bf16)
            prob = prob.astype(bf16)
            p_all[:, lane] = prob
            ds_all[:, lane] = dscore
            att = mm(vtw[chan, :], prob).astype(bf16)
            att_s[low, cols] = att[:head_dim, :BLOCK]
            att_s[high, cols] = att[head_dim:, BLOCK:]
            gq = mm(ktw[chan, :], dscore) * scale
            gq_s[low, cols] = gq[:head_dim, :BLOCK]
            gq_s[high, cols] = gq[head_dim:, BLOCK:]
        gk = mm(ds_all[...], qbd[...], NT)
        gk_s[span, :] += gk[:WINDOW]
        gk_s[near:, :] += gk[WINDOW:]
        gv = mm(p_all[...], gbd[...], NT)
        gv_s[span, :] += gv[:WINDOW]
        gv_s[near:, :] += gv[WINDOW:]
        return carry

    lax.fori_loop(0, rows // BLOCK, block, 0)

    gkt = (gk_s[...] * scale).T.astype(bf16)
    gvt = gv_s[...].T.astype(bf16)
    gq = pltpu.roll(gq_s[...], MARGIN, 1).astype(bf16)
    d_all = mm(weight(1), gkt, TN) + mm(weight(2), gvt, TN)
    out[:, :near] = (d_all[:, :near] + mm(weight(0), gq, TN)).astype(bf16)
    out[:, near:keys] = d_all[:, near:].astype(bf16)
    parts = (
        mm(gq, recv[:, :near], NT),
        mm(gkt, recv[:, :keys], NT),
        mm(gvt, recv[:, :keys], NT),
        mm(att_s[...], recv[:, at_dy : at_dy + rows], NT),
    )
    for t, part in enumerate(parts):
        out[:, keys + t * C : keys + (t + 1) * C] = (part * grad_scale).astype(bf16)


def local(tokens, grad_in, w_qkv, w_out, neighbors, send_rows):
    groups = lax.axis_size("tile")
    head_count = lax.axis_size("head")
    border = send_rows.shape[2]
    offsets = (1, groups - 1, groups // 2)
    share, full_rows = tokens.shape
    rows = full_rows // head_count
    near = rows + 2 * MARGIN
    keys = near + 3 * border
    wide = WINDOW + 3 * border
    bf16 = jnp.bfloat16

    flat = send_rows[0].reshape(-1)
    chosen = (lax.broadcasted_iota(jnp.int32, (full_rows, 3 * border), 0) == flat[None, :]).astype(bf16)
    mine = jnp.dot(tokens, chosen, preferred_element_type=jnp.float32).astype(bf16)
    theirs = [
        passed_along(mine[:, p * border : (p + 1) * border], "tile", offsets[p]) for p in range(3)
    ]
    ext = jnp.concatenate([tokens[:, full_rows - MARGIN :], tokens, tokens[:, :MARGIN]], axis=1)
    weights = [w_qkv[0], w_qkv[1], w_qkv[2], w_out]
    sends = jnp.stack(
        [
            jnp.concatenate(
                [ext[:, h * rows : h * rows + near]]
                + theirs
                + [grad_in[:, h * rows : (h + 1) * rows]]
                + weights,
                axis=1,
            )
            for h in range(head_count)
        ]
    )
    recv = lax.all_to_all(sends, "head", split_axis=0, concat_axis=0, tiled=True)
    recv = recv.reshape(C, sends.shape[2])

    start_row = lax.axis_index("head") * rows
    near_ids = lax.dynamic_slice_in_dim(neighbors, start_row, rows, 1)
    block_start = (jnp.arange(rows, dtype=jnp.int32) // BLOCK) * BLOCK
    picks = jnp.where(
        near_ids < full_rows,
        (near_ids - start_row + MARGIN) % full_rows - block_start[None, :],
        near_ids - full_rows + WINDOW,
    )
    grad_scale = 1.0 / math.sqrt(full_rows * groups)
    vm = pltpu.VMEM
    width = keys + 4 * C
    result = pl.pallas_call(
        functools.partial(attention_body, rows, near, keys, grad_scale),
        out_shape=jax.ShapeDtypeStruct((C, width), bf16),
        in_specs=[pl.BlockSpec(memory_space=vm)] * 2,
        out_specs=pl.BlockSpec(memory_space=vm),
        scratch_shapes=[
            vm((C, rows), bf16),
            vm((C, rows), bf16),
            vm((keys, C), bf16),
            vm((C, keys), bf16),
            vm((keys, C), bf16),
            vm((C, keys), bf16),
            vm((wide, C), bf16),
            vm((C, wide), bf16),
            vm((wide, C), bf16),
            vm((C, wide), bf16),
            vm((C, HEADS * BLOCK), bf16),
            vm((C, HEADS * BLOCK), bf16),
            vm((wide, HEADS * BLOCK), bf16),
            vm((wide, HEADS * BLOCK), bf16),
            vm((keys, C), jnp.float32),
            vm((keys, C), jnp.float32),
            vm((C, rows), bf16),
            vm((C, near), jnp.float32),
        ],
        compiler_params=pltpu.CompilerParams(vmem_limit_bytes=56 * 1024 * 1024),
        name="attend",
    )(recv, picks)

    back = lax.all_to_all(
        result.reshape(head_count, share, width), "head", split_axis=0, concat_axis=0, tiled=True
    )
    returned = jnp.sum(back[:, :, near:keys].astype(jnp.float32), axis=0).astype(bf16)
    answers = [
        passed_along(
            returned[:, p * border : (p + 1) * border], "tile", (groups - offsets[p]) % groups
        )
        for p in range(3)
    ]
    partial = jnp.sum(back[:, :, keys:].astype(jnp.float32), axis=0).astype(bf16)
    pieces = lax.all_to_all(
        partial.reshape(groups, -1), "tile", split_axis=0, concat_axis=0, tiled=True
    )
    piece = jnp.sum(pieces.astype(jnp.float32), axis=0).astype(bf16)
    gathered = lax.all_to_all(
        jnp.broadcast_to(piece[None, :], pieces.shape), "tile", split_axis=0, concat_axis=0, tiled=True
    )
    totals = gathered.reshape(share, 4, C).astype(jnp.float32)
    grad_qkv = totals[:, :3].transpose(1, 0, 2)
    grad_out = totals[:, 3]

    gap = jnp.zeros((share, rows - 2 * MARGIN), bf16)
    own = jnp.concatenate([back[h, :, MARGIN : MARGIN + rows] for h in range(head_count)], axis=1)
    edges = jnp.concatenate(
        [
            part
            for h in range(head_count)
            for part in (
                back[(h - 1) % head_count, :, near - MARGIN : near],
                gap,
                back[(h + 1) % head_count, :, :MARGIN],
            )
        ],
        axis=1,
    )
    spread = lax.dot_general(
        jnp.concatenate(answers, axis=1), chosen, NT, preferred_element_type=jnp.float32
    )
    d_tokens = (
        grad_in.astype(jnp.float32) + own.astype(jnp.float32) + edges.astype(jnp.float32) + spread
    )
    return (d_tokens, grad_qkv, grad_out)


def solution(mesh):
    return jax.shard_map(
        local,
        mesh=mesh,
        in_specs=(
            P("head", "tile"),
            P("head", "tile"),
            P(None, "head", None),
            P("head", None),
            P(None, "tile"),
            P("tile", None, None),
        ),
        out_specs=(P("head", "tile"), P(None, "head", None), P("head", None)),
        check_vma=False,
    )
```

```python
import functools
import math

import jax
import jax.numpy as jnp
from jax import lax
from jax.experimental import pallas as pl
from jax.experimental.pallas import tpu as pltpu
from jax.sharding import PartitionSpec as P

C = 256
HEADS = 8
NBR = 9
MARGIN = 64
BLOCK = 2 * MARGIN
WINDOW = 2 * BLOCK
NEVER = -1.0e30

NT = (((1,), (1,)), ((), ()))
TN = (((0,), (0,)), ((), ()))


def mm(a, b, dims=(((1,), (0,)), ((), ()))):
    return lax.dot_general(a, b, dims, preferred_element_type=jnp.float32)


def attention_body(
    rows, near, keys, grad_scale,
    recv, picks, out,
    q_s, g_s, k_s, kt_s, v_s, vt_s, kw, ktw, vw, vtw, qbd, gbd, p_all, ds_all, gk_s, gv_s, att_s, gq_s,
):
    head_dim = C // HEADS
    scale = 1.0 / math.sqrt(head_dim)
    scale2 = scale / math.log(2.0)
    wide = keys - near + WINDOW
    at_x = rows
    at_w = rows + keys
    bf16 = jnp.bfloat16

    def weight(t):
        return recv[:, at_w + t * C : at_w + (t + 1) * C]

    q_ext = mm(weight(0), recv[:, at_x : at_x + near])
    q_s[...] = pltpu.roll(q_ext, near - MARGIN, 1)[:, :rows].astype(bf16)
    g_s[...] = mm(weight(3), recv[:, :rows]).astype(bf16)
    kt = mm(weight(1), recv[:, at_x : at_x + keys])
    kt_s[...] = kt.astype(bf16)
    k_s[...] = kt.T.astype(bf16)
    vt = mm(weight(2), recv[:, at_x : at_x + keys])
    vt_s[...] = vt.astype(bf16)
    v_s[...] = vt.T.astype(bf16)
    kw[WINDOW:, :] = k_s[near:, :]
    vw[WINDOW:, :] = v_s[near:, :]
    ktw[:, WINDOW:] = kt_s[:, near:]
    vtw[:, WINDOW:] = vt_s[:, near:]
    qbd[...] = jnp.zeros_like(qbd)
    gbd[...] = jnp.zeros_like(gbd)
    gk_s[...] = jnp.zeros_like(gk_s)
    gv_s[...] = jnp.zeros_like(gv_s)
    gq_s[:, rows:] = jnp.zeros((C, near - rows), jnp.float32)

    def block(b, carry):
        start = pl.multiple_of(b * BLOCK, BLOCK)
        cols = pl.ds(start, BLOCK)
        span = pl.ds(start, WINDOW)
        kw[:WINDOW, :] = k_s[span, :]
        vw[:WINDOW, :] = v_s[span, :]
        ktw[:, :WINDOW] = kt_s[:, span]
        vtw[:, :WINDOW] = vt_s[:, span]
        for h in range(HEADS):
            chan = slice(h * head_dim, (h + 1) * head_dim)
            lane = slice(h * BLOCK, (h + 1) * BLOCK)
            qbd[chan, lane] = q_s[chan, cols]
            gbd[chan, lane] = g_s[chan, cols]
        ids = lax.broadcasted_iota(jnp.int32, (wide, BLOCK), 0)
        count = jnp.zeros((wide, BLOCK), jnp.float32)
        for j in range(NBR):
            count = count + jnp.where(ids == picks[j : j + 1, cols], 1.0, 0.0)
        bias = jnp.where(count > 0.0, jnp.log2(jnp.maximum(count, 1.0)), NEVER)
        bias = jnp.concatenate([bias, bias], axis=1)
        for pair in range(HEADS // 2):
            lane = slice(pair * 2 * BLOCK, (pair + 1) * 2 * BLOCK)
            chan = slice(pair * 2 * head_dim, (pair + 1) * 2 * head_dim)
            low = slice(pair * 2 * head_dim, pair * 2 * head_dim + head_dim)
            high = slice(pair * 2 * head_dim + head_dim, (pair + 1) * 2 * head_dim)
            expon = jnp.exp2(mm(kw[...], qbd[:, lane]) * scale2 + bias)
            total = jnp.sum(expon, axis=0, keepdims=True)
            prob = expon * (1.0 / total)
            dprob = mm(vw[...], gbd[:, lane])
            mean = jnp.sum(prob * dprob, axis=0, keepdims=True)
            dscore = (prob * (dprob - mean)).astype(bf16)
            prob = prob.astype(bf16)
            p_all[:, lane] = prob
            ds_all[:, lane] = dscore
            att = mm(vtw[chan, :], prob).astype(bf16)
            att_s[low, cols] = att[:head_dim, :BLOCK]
            att_s[high, cols] = att[head_dim:, BLOCK:]
            gq = mm(ktw[chan, :], dscore) * scale
            gq_s[low, cols] = gq[:head_dim, :BLOCK]
            gq_s[high, cols] = gq[head_dim:, BLOCK:]
        gk = mm(ds_all[...], qbd[...], NT)
        gk_s[span, :] += gk[:WINDOW]
        gk_s[near:, :] += gk[WINDOW:]
        gv = mm(p_all[...], gbd[...], NT)
        gv_s[span, :] += gv[:WINDOW]
        gv_s[near:, :] += gv[WINDOW:]
        return carry

    lax.fori_loop(0, rows // BLOCK, block, 0)

    gkt = (gk_s[...] * scale).T.astype(bf16)
    gvt = gv_s[...].T.astype(bf16)
    gq = pltpu.roll(gq_s[...], MARGIN, 1).astype(bf16)
    d_all = mm(weight(1), gkt, TN) + mm(weight(2), gvt, TN)
    out[:, :near] = (d_all[:, :near] + mm(weight(0), gq, TN)).astype(bf16)
    out[:, near:keys] = d_all[:, near:].astype(bf16)
    parts = (
        mm(gq, recv[:, at_x : at_x + near], NT),
        mm(gkt, recv[:, at_x : at_x + keys], NT),
        mm(gvt, recv[:, at_x : at_x + keys], NT),
        mm(att_s[...], recv[:, :rows], NT),
    )
    for t, part in enumerate(parts):
        out[:, keys + t * C : keys + (t + 1) * C] = (part * grad_scale).astype(bf16)


def on_mesh(tile, head):
    return {"tile": tile, "head": head}


def greet(peers):
    barrier = pltpu.get_barrier_semaphore()
    for peer in peers:
        pl.semaphore_signal(barrier, inc=1, device_id=peer, device_id_type=pl.DeviceIdType.MESH)
    pl.semaphore_wait(barrier, len(peers))


def send(src, dst, send_sem, recv_sem, peer):
    copy = pltpu.make_async_remote_copy(
        src_ref=src,
        dst_ref=dst,
        send_sem=send_sem,
        recv_sem=recv_sem,
        device_id=peer,
        device_id_type=pl.DeviceIdType.MESH,
    )
    copy.start()
    return copy


def exchange_in(
    groups, heads, share, border, body, keys, pieces, mine, w, recv,
    halo, w_send, w_recv, wf_send, wf_recv, p_send, p_recv, b_send, b_recv, bf_send, bf_recv, l_send, l_recv,
):
    tile, me = lax.axis_index("tile"), lax.axis_index("head")
    offsets = (1, groups - 1, groups // 2)
    partner = (me // 2) * 2 + 1 - me % 2
    at_b, at_w = body, body + 3 * border
    full = recv.shape[1]

    def rows_of(index):
        return pl.ds(pl.multiple_of(index * share, share), share)

    greet(
        [on_mesh(tile, (me + k) % heads) for k in range(1, heads)]
        + [on_mesh((tile + step) % groups, me) for step in offsets]
    )
    lists = [
        send(mine.at[p], halo.at[p], l_send.at[p], l_recv.at[p], on_mesh((tile + offsets[p]) % groups, me))
        for p in range(3)
    ]
    steps = range(2, heads, 2)
    w_here = recv.at[rows_of(me), at_w:full]
    w_copies = [
        send(w, w_here, w_send.at[i], w_recv.at[i], on_mesh(tile, (me + k) % heads))
        for i, k in enumerate(steps)
    ]
    w_near = send(w, w_here, w_send.at[len(steps)], w_recv.at[len(steps)], on_mesh(tile, partner))
    sends = []
    for k in range(1, heads):
        to = (me + k) % heads
        sends.append(
            send(pieces.at[to], recv.at[rows_of(me), 0:body], p_send.at[k - 1], p_recv.at[k - 1], on_mesh(tile, to))
        )
    recv[rows_of(me), 0:body] = pieces[me]
    recv[rows_of(me), at_w:full] = w[...]
    for copy in lists:
        copy.wait()
    b_copies = []
    for p in range(3):
        cols = slice(at_b + p * border, at_b + (p + 1) * border)
        for i, k in enumerate(steps):
            b_copies.append(
                send(halo.at[p], recv.at[rows_of(me), cols], b_send.at[p, i], b_recv.at[p, i], on_mesh(tile, (me + k) % heads))
            )
        b_copies.append(
            send(halo.at[p], recv.at[rows_of(me), cols], b_send.at[p, len(steps)], b_recv.at[p, len(steps)], on_mesh(tile, partner))
        )
        recv[rows_of(me), cols] = halo[p]
    last = []
    for i, k in enumerate(steps):
        w_copies[i].wait()
        block = recv.at[rows_of((me + heads - k) % heads), at_w:full]
        last.append(send(block, block, wf_send.at[i], wf_recv.at[i], on_mesh(tile, partner)))
    w_near.wait()
    for copy in b_copies:
        copy.wait()
    for i, k in enumerate(steps):
        block = recv.at[rows_of((me + heads - k) % heads), at_b:at_w]
        last.append(send(block, block, bf_send.at[i], bf_recv.at[i], on_mesh(tile, partner)))
    for copy in sends + last:
        copy.wait()


def exchange_out(
    groups, heads, share, border, near, keys, result, own, answers, totals,
    dwr, br, s1, rs, ansb, w_send, w_recv, b_send, b_recv, d_send, d_recv, r_send, r_recv, g_send, g_recv, a_send, a_recv,
):
    tile, me = lax.axis_index("tile"), lax.axis_index("head")
    offsets = (1, groups - 1, groups // 2)
    full = result.shape[1]
    depth = s1.shape[1]
    blocks = (full - keys) // 128

    def rows_of(index):
        return pl.ds(pl.multiple_of(index * share, share), share)

    others = [(me + k) % heads for k in range(1, heads)]
    peers = [(tile + k) % groups for k in range(1, groups)]
    greet([on_mesh(tile, to) for to in others] + [on_mesh(to, me) for to in peers])
    w_copies = [
        send(result.at[rows_of(to), keys:full], dwr.at[i], w_send.at[i], w_recv.at[i], on_mesh(tile, to))
        for i, to in enumerate(others)
    ]
    b_copies = [
        send(result.at[rows_of(to), near:keys], br.at[i], b_send.at[i], b_recv.at[i], on_mesh(tile, to))
        for i, to in enumerate(others)
    ]
    d_copies = [
        send(result.at[rows_of(to), 0:near], own.at[me], d_send.at[i], d_recv.at[i], on_mesh(tile, to))
        for i, to in enumerate(others)
    ]
    own[me] = result[rows_of(me), 0:near]
    for copy in w_copies:
        copy.wait()
    total = result[rows_of(me), keys:full].astype(jnp.float32)
    for i in range(heads - 1):
        total = total + dwr[i].astype(jnp.float32)
    for g in range(groups):
        row, col = (g // blocks) * depth, (g % blocks) * 128
        s1[g] = total[row : row + depth, col : col + 128].astype(jnp.bfloat16)
    r_copies = [
        send(s1.at[to], rs.at[i], r_send.at[i], r_recv.at[i], on_mesh(to, me)) for i, to in enumerate(peers)
    ]
    for copy in b_copies:
        copy.wait()
    back = result[rows_of(me), near:keys].astype(jnp.float32)
    for i in range(heads - 1):
        back = back + br[i].astype(jnp.float32)
    for p in range(3):
        ansb[p] = back[:, p * border : (p + 1) * border].astype(jnp.bfloat16)
    a_copies = [
        send(ansb.at[p], answers.at[p], a_send.at[p], a_recv.at[p], on_mesh((tile + groups - offsets[p]) % groups, me))
        for p in range(3)
    ]
    for copy in r_copies:
        copy.wait()
    piece = s1[tile].astype(jnp.float32)
    for i in range(groups - 1):
        piece = piece + rs[i].astype(jnp.float32)
    totals[tile] = piece.astype(jnp.bfloat16)
    g_copies = [
        send(totals.at[tile], totals.at[tile], g_send.at[i], g_recv.at[i], on_mesh(to, me))
        for i, to in enumerate(peers)
    ]
    for copy in a_copies + g_copies + d_copies:
        copy.wait()


def local(tokens, grad_in, w_qkv, w_out, neighbors, send_rows):
    groups = lax.axis_size("tile")
    head_count = lax.axis_size("head")
    border = send_rows.shape[2]
    offsets = (1, groups - 1, groups // 2)
    share, full_rows = tokens.shape
    rows = full_rows // head_count
    near = rows + 2 * MARGIN
    keys = near + 3 * border
    wide = WINDOW + 3 * border
    bf16 = jnp.bfloat16

    flat = send_rows[0].reshape(-1)
    chosen = (lax.broadcasted_iota(jnp.int32, (full_rows, 3 * border), 0) == flat[None, :]).astype(bf16)
    mine = jnp.dot(tokens, chosen, preferred_element_type=jnp.float32).astype(bf16)
    mine = mine.reshape(share, 3, border).transpose(1, 0, 2)
    ext = jnp.concatenate([tokens[:, full_rows - MARGIN :], tokens, tokens[:, :MARGIN]], axis=1)
    weights = jnp.concatenate([w_qkv[0], w_qkv[1], w_qkv[2], w_out], axis=1)
    sends = jnp.stack(
        [
            jnp.concatenate(
                [grad_in[:, h * rows : (h + 1) * rows], ext[:, h * rows : h * rows + near]], axis=1
            )
            for h in range(head_count)
        ]
    )
    vm = pltpu.VMEM
    dma = pltpu.SemaphoreType.DMA
    far = (head_count - 1) // 2
    recv = pl.pallas_call(
        functools.partial(exchange_in, groups, head_count, share, border, rows + near, keys),
        out_shape=jax.ShapeDtypeStruct((C, rows + keys + 4 * C), bf16),
        in_specs=[pl.BlockSpec(memory_space=vm)] * 3,
        out_specs=pl.BlockSpec(memory_space=vm),
        scratch_shapes=[
            vm((3, share, border), bf16),
            dma((far + 1,)), dma((far + 1,)), dma((far,)), dma((far,)),
            dma((head_count - 1,)), dma((head_count - 1,)),
            dma((3, far + 1)), dma((3, far + 1)), dma((far,)), dma((far,)),
            dma((3,)), dma((3,)),
        ],
        compiler_params=pltpu.CompilerParams(
            collective_id=0, has_side_effects=True, vmem_limit_bytes=24 * 1024 * 1024
        ),
        name="exchange_in",
    )(sends, mine, weights)

    start_row = lax.axis_index("head") * rows
    near_ids = lax.dynamic_slice_in_dim(neighbors, start_row, rows, 1)
    block_start = (jnp.arange(rows, dtype=jnp.int32) // BLOCK) * BLOCK
    picks = jnp.where(
        near_ids < full_rows,
        (near_ids - start_row + MARGIN) % full_rows - block_start[None, :],
        near_ids - full_rows + WINDOW,
    )
    grad_scale = 1.0 / math.sqrt(full_rows * groups)
    width = keys + 4 * C
    result = pl.pallas_call(
        functools.partial(attention_body, rows, near, keys, grad_scale),
        out_shape=jax.ShapeDtypeStruct((C, width), bf16),
        in_specs=[pl.BlockSpec(memory_space=vm)] * 2,
        out_specs=pl.BlockSpec(memory_space=vm),
        scratch_shapes=[
            vm((C, rows), bf16),
            vm((C, rows), bf16),
            vm((keys, C), bf16),
            vm((C, keys), bf16),
            vm((keys, C), bf16),
            vm((C, keys), bf16),
            vm((wide, C), bf16),
            vm((C, wide), bf16),
            vm((wide, C), bf16),
            vm((C, wide), bf16),
            vm((C, HEADS * BLOCK), bf16),
            vm((C, HEADS * BLOCK), bf16),
            vm((wide, HEADS * BLOCK), bf16),
            vm((wide, HEADS * BLOCK), bf16),
            vm((keys, C), jnp.float32),
            vm((keys, C), jnp.float32),
            vm((C, rows), bf16),
            vm((C, near), jnp.float32),
        ],
        compiler_params=pltpu.CompilerParams(vmem_limit_bytes=56 * 1024 * 1024),
        name="attend",
    )(recv, picks)

    depth = share * 4 * C // 128 // groups
    others, peers = head_count - 1, groups - 1
    back, answers, totals = pl.pallas_call(
        functools.partial(exchange_out, groups, head_count, share, border, near, keys),
        out_shape=(
            jax.ShapeDtypeStruct((head_count, share, near), bf16),
            jax.ShapeDtypeStruct((3, share, border), bf16),
            jax.ShapeDtypeStruct((groups, depth, 128), bf16),
        ),
        in_specs=[pl.BlockSpec(memory_space=vm)],
        out_specs=[pl.BlockSpec(memory_space=vm)] * 3,
        scratch_shapes=[
            vm((others, share, 4 * C), bf16),
            vm((others, share, 3 * border), bf16),
            vm((groups, depth, 128), bf16),
            vm((peers, depth, 128), bf16),
            vm((3, share, border), bf16),
        ]
        + [dma((others,))] * 6
        + [dma((peers,))] * 4
        + [dma((3,))] * 2,
        compiler_params=pltpu.CompilerParams(
            collective_id=1, has_side_effects=True, vmem_limit_bytes=24 * 1024 * 1024
        ),
        name="exchange_out",
    )(result)
    blocks = 4 * C // 128
    totals = totals.reshape(groups // blocks, blocks, depth, 128).transpose(0, 2, 1, 3)
    totals = totals.reshape(share, 4, C).astype(jnp.float32)
    grad_qkv = totals[:, :3].transpose(1, 0, 2)
    grad_out = totals[:, 3]

    gap = jnp.zeros((share, rows - 2 * MARGIN), bf16)
    own = jnp.concatenate([back[h, :, MARGIN : MARGIN + rows] for h in range(head_count)], axis=1)
    edges = jnp.concatenate(
        [
            part
            for h in range(head_count)
            for part in (
                back[(h - 1) % head_count, :, near - MARGIN : near],
                gap,
                back[(h + 1) % head_count, :, :MARGIN],
            )
        ],
        axis=1,
    )
    spread = lax.dot_general(
        answers.transpose(1, 0, 2).reshape(share, 3 * border), chosen, NT, preferred_element_type=jnp.float32
    )
    d_tokens = (
        grad_in.astype(jnp.float32) + own.astype(jnp.float32) + edges.astype(jnp.float32) + spread
    )
    return (d_tokens, grad_qkv, grad_out)


def solution(mesh):
    return jax.shard_map(
        local,
        mesh=mesh,
        in_specs=(
            P("head", "tile"),
            P("head", "tile"),
            P(None, "head", None),
            P("head", None),
            P(None, "tile"),
            P("tile", None, None),
        ),
        out_specs=(P("head", "tile"), P(None, "head", None), P("head", None)),
        check_vma=False,
    )
```
